32 devices in a mesh: group: 4 (over y, x), member: 8 (over z, core).
Axes of the slice: x: 2, y: 2, z: 4, core: 2. Of those that a mesh axis runs over, the one named last changes fastest.
Arguments:
- load: float32 [3, 7, 7, 8, 4096], P(None, None, None, None, ('group', 'member')), may hold values from -6 to 6
- stiffness_dir: float32 [3, 4096], P(None, ('group', 'member')), may hold values from 0.5 to 4
- bulk_ratio: float32 [4096], P(('group', 'member')), may hold values from 0 to 2
- thermal_shift: float32 [4096], P(('group', 'member')), may hold values from 0.5 to 5
- contact: int32 [2, 7, 7, 4096], P(None, None, None, ('group', 'member')), may hold values 0 or 1
- loop_tie: float32 [4096], P(('group', 'member')), may hold values from 0.5 to 4
Outputs:
- solution: float32 [3, 7, 7, 8, 4096], P(None, None, None, None, ('group', 'member'))
- residual: float32 [3, 7, 7, 8, 4096], P(None, None, None, None, ('group', 'member'))
The draws below stay inside these ranges and needn't reach their ends.
All inputs are finite; a program needn't handle non-finite values. No bound on the sum of `contact` on one device may be relied on, other than what follows from the above.
Results may differ from the reference program's by a relative error of at most 0.0003.
Values sent between devices are 32-bit elements; how exact they have to be, the bound alone decides.
No kernel may reach another device: no remote copies, remote signals or barrier semaphores. Data moves between devices by JAX's collectives and lax.ppermute only.
A program may use at most 128 MiB of HBM per device.

```python
import math
import jax
import jax.numpy as jnp
import numpy as np
from jax import lax

NODES = 8
MID_NODES = 4
COARSE_NODES = 2
SWEEPS = 2
CHEB = 6
E_DEV = 128
OWNED = 7
ELEMS = 4096
N_GROUP = 4
N_MEMBER = 8


def place_ends(entries, own_key, low, high):
    extent = entries.shape
    index_at = [jax.random.randint(jax.random.fold_in(own_key, axis), (), 0, extent[axis]) for axis in range(len(extent))]
    entries = entries.at[tuple(index_at)].set(low)
    longest = extent.index(max(extent))
    index_at[longest] = (index_at[longest] + 1) % extent[longest]
    return entries.at[tuple(index_at)].set(high)


def level_of(stream_key, extent, pieces, low, top_value):
    def one(dim, parts):
        heights = jax.random.uniform(jax.random.fold_in(jax.random.fold_in(stream_key, 6), dim), (parts,), jnp.float32, low / len(pieces), top_value / len(pieces))
        return jnp.repeat(jnp.exp(heights), extent[dim] // parts).reshape((-1,) + (1,) * (len(extent) - dim - 1))

    gain = one(*pieces[0])
    for cut in pieces[1:]:
        gain = gain * one(*cut)
    return gain


def noise(stream_key, shape, spread, limit, split=(), dtype=jnp.bfloat16):
    entries = spread * jax.random.normal(stream_key, shape, jnp.float32)
    if split:
        entries = entries * level_of(stream_key, shape, split, -0.22, 0.18)
    return jnp.clip(entries, -limit, limit).astype(dtype)


def setup_inputs(seed: int = 0) -> dict:
    streams_of = jax.random.split(jax.random.key(seed), 7)
    load = noise(streams_of[0], (3, OWNED, OWNED, NODES, ELEMS), 1.0, 6.0, ((4, 32),), jnp.float32)
    stiffness_dir = jnp.clip(jnp.exp(math.log(4.0) - 2.0794415 * jax.random.uniform(streams_of[1], (3, ELEMS), jnp.float32) ** level_of(streams_of[1], (3, ELEMS), ((1, 32),), -0.2, 0.2)), 0.5, 4.0)
    bulk_ratio = jnp.clip(2.0 * jax.random.uniform(streams_of[2], (ELEMS,), jnp.float32) ** level_of(streams_of[2], (ELEMS,), ((0, 32),), -0.2, 0.2), 0.0, 2.0)
    thermal_shift = jnp.clip(jnp.exp(math.log(5.0) - 2.3025851 * jax.random.uniform(streams_of[3], (ELEMS,), jnp.float32) ** level_of(streams_of[3], (ELEMS,), ((0, 32),), -0.2, 0.2)), 0.5, 5.0)
    contact = place_ends((jax.random.randint(streams_of[4], (2, OWNED, OWNED, ELEMS), 0, 3) < 1).astype(jnp.int32), jax.random.fold_in(streams_of[4], 1), 0, 1)
    loop_tie = jnp.clip(jnp.exp(math.log(4.0) - 2.0794415 * jax.random.uniform(streams_of[5], (ELEMS,), jnp.float32) ** level_of(streams_of[5], (ELEMS,), ((0, 32),), -0.2, 0.2)), 0.5, 4.0)
    return {"load": load, "stiffness_dir": stiffness_dir, "bulk_ratio": bulk_ratio, "thermal_shift": thermal_shift, "contact": contact, "loop_tie": loop_tie}


OMEGA = 0.3
LOWER_BOUND = 0.3
UPPER_BOUND = 3.0
HIGHEST = lax.Precision.HIGHEST


def tables(resolution):
    indices = np.arange(resolution)
    points = -np.cos(np.pi * indices / (resolution - 1))
    padded = np.concatenate([points[:1], points, points[-1:]])
    weights = (padded[2:] - padded[:-2]) / 2.0
    factor = np.where((indices == 0) | (indices == resolution - 1), 2.0, 1.0)
    spacing = points[:, None] - points[None, :] + np.eye(resolution)
    parity = np.where((indices[:, None] + indices[None, :]) % 2 == 0, 1.0, -1.0)
    offdiag = (1.0 - np.eye(resolution)) * factor[:, None] / factor[None, :] * parity / spacing
    derivative = offdiag - np.eye(resolution) * offdiag.sum(axis=1)[:, None]
    stiffness = (weights[:, None] * derivative * derivative).sum(axis=0)
    return points, weights, derivative, stiffness


def interpolation(fine_count, coarse_count):
    fine_points = tables(fine_count)[0]
    coarse_points = tables(coarse_count)[0]
    columns = []
    for column in range(coarse_count):
        values = np.ones(fine_count)
        for partner in range(coarse_count):
            if partner != column:
                values = values * (fine_points - coarse_points[partner]) / (coarse_points[column] - coarse_points[partner])
        columns.append(values)
    return jnp.asarray(np.stack(columns, axis=1), jnp.float32)


def cube_shape(resolution, extra):
    return (resolution, resolution, resolution) + (1,) * extra


def tensor(first, second, third, resolution, extra):
    return (first[:, None, None] * second[None, :, None] * third[None, None, :]).reshape(cube_shape(resolution, extra))


def element_apply(displace, coefficients, resolution):
    moduli, bulk, reaction = coefficients
    weight = jnp.asarray(tables(resolution)[1], jnp.float32)
    matrix = jnp.asarray(tables(resolution)[2], jnp.float32)
    volume = tensor(weight, weight, weight, resolution, displace.ndim - 4)
    mixed = displace + bulk * jnp.sum(displace, axis=0, keepdims=True) / 3.0
    result = reaction * volume * displace
    first = jnp.einsum("ai,cijk...->cajk...", matrix, mixed, precision=HIGHEST)
    result = result + jnp.einsum("ai,cajk...->cijk...", matrix, moduli[0] * volume * first, precision=HIGHEST)
    second = jnp.einsum("aj,cijk...->ciak...", matrix, mixed, precision=HIGHEST)
    result = result + jnp.einsum("aj,ciak...->cijk...", matrix, moduli[1] * volume * second, precision=HIGHEST)
    third = jnp.einsum("ak,cijk...->cija...", matrix, mixed, precision=HIGHEST)
    result = result + jnp.einsum("ak,cija...->cijk...", matrix, moduli[2] * volume * third, precision=HIGHEST)
    return result


def element_diagonal(coefficients, resolution):
    moduli, bulk, reaction = coefficients
    weight = jnp.asarray(tables(resolution)[1], jnp.float32)
    stiffness = jnp.asarray(tables(resolution)[3], jnp.float32)
    extra = bulk.ndim
    value = (1.0 + bulk / 3.0) * (moduli[0] * tensor(stiffness, weight, weight, resolution, extra) + moduli[1] * tensor(weight, stiffness, weight, resolution, extra) + moduli[2] * tensor(weight, weight, stiffness, resolution, extra)) + reaction * tensor(weight, weight, weight, resolution, extra)
    return jnp.broadcast_to(value[None], (3,) + value.shape)


def extend(owned, moves):
    along_next, across_next, along_prev, across_prev = moves
    layer = along_next(owned[:, 0])
    wider = jnp.concatenate([owned, layer[:, None]], axis=1)
    column = across_next(wider[:, :, 0])
    return jnp.concatenate([wider, column[:, :, None]], axis=2)


def fold(full, moves):
    along_next, across_next, along_prev, across_prev = moves
    boundary = full.shape[2] - 1
    folded = jnp.concatenate([full[:, :, :1] + across_prev(full[:, :, boundary])[:, :, None], full[:, :, 1:boundary]], axis=2)
    return jnp.concatenate([folded[:, :1] + along_prev(folded[:, boundary])[:, None], folded[:, 1:boundary]], axis=1)


def level_apply(owned, coefficients, resolution, moves):
    return fold(element_apply(extend(owned, moves), coefficients, resolution), moves)


def level_diagonal(coefficients, resolution, moves):
    return fold(element_diagonal(coefficients, resolution), moves)


def prolong(coarse, matrix, moves):
    full = extend(coarse, moves)
    full = jnp.einsum("fi,cijk...->cfjk...", matrix, full, precision=HIGHEST)
    full = jnp.einsum("fj,cijk...->cifk...", matrix, full, precision=HIGHEST)
    full = jnp.einsum("fk,cijk...->cijf...", matrix, full, precision=HIGHEST)
    boundary = matrix.shape[0] - 1
    return full[:, :boundary, :boundary]


def restrict(fine, matrix, moves):
    wider = jnp.concatenate([fine, jnp.zeros_like(fine[:, :1])], axis=1)
    full = jnp.concatenate([wider, jnp.zeros_like(wider[:, :, :1])], axis=2)
    full = jnp.einsum("fi,cfjk...->cijk...", matrix, full, precision=HIGHEST)
    full = jnp.einsum("fj,cifk...->cijk...", matrix, full, precision=HIGHEST)
    full = jnp.einsum("fk,cijf...->cijk...", matrix, full, precision=HIGHEST)
    return fold(full, moves)


def free_mask(contact_float, resolution):
    middle = jnp.ones(contact_float.shape[1:3] + (resolution - 2,) + contact_float.shape[3:], jnp.float32)
    return jnp.concatenate([(1.0 - contact_float[0])[:, :, None], middle, (1.0 - contact_float[1])[:, :, None]], axis=2)


def smooth(iterate, rhs, operator, inverse, sweeps):
    for repeat in range(sweeps):
        iterate = iterate + OMEGA * inverse * (rhs - operator(iterate))
    return iterate


def chebyshev(rhs, operator, inverse):
    center = 0.5 * (UPPER_BOUND + LOWER_BOUND)
    radius = 0.5 * (UPPER_BOUND - LOWER_BOUND)
    ratio = center / radius
    damping_now = 1.0 / ratio
    remain = rhs
    update = inverse * remain / center
    iterate = jnp.zeros_like(rhs)
    for iteration in range(CHEB):
        iterate = iterate + update
        if iteration + 1 < CHEB:
            remain = remain - operator(update)
            damping_next = 1.0 / (2.0 * ratio - damping_now)
            update = damping_next * damping_now * update + (2.0 * damping_next / radius) * inverse * remain
            damping_now = damping_next
    return iterate


def vcycle(load, coefficients, freedom, moves, coarse_solve):
    fine_mid = interpolation(NODES, MID_NODES)
    mid_coarse = interpolation(MID_NODES, COARSE_NODES)

    def apply_fine(values):
        return freedom * level_apply(values, coefficients, NODES, moves)

    def apply_mid(values):
        return level_apply(values, coefficients, MID_NODES, moves)

    inverse_fine = freedom / level_diagonal(coefficients, NODES, moves)
    inverse_mid = 1.0 / level_diagonal(coefficients, MID_NODES, moves)
    rhs_fine = freedom * load
    fine_iter = smooth(OMEGA * inverse_fine * rhs_fine, rhs_fine, apply_fine, inverse_fine, SWEEPS - 1)
    rhs_mid = restrict(rhs_fine - apply_fine(fine_iter), fine_mid, moves)
    mid_iter = smooth(OMEGA * inverse_mid * rhs_mid, rhs_mid, apply_mid, inverse_mid, SWEEPS - 1)
    rhs_coarse = restrict(rhs_mid - apply_mid(mid_iter), mid_coarse, moves)
    coarse_iter = coarse_solve(rhs_coarse)
    mid_iter = smooth(mid_iter + prolong(coarse_iter, mid_coarse, moves), rhs_mid, apply_mid, inverse_mid, SWEEPS)
    fine_iter = smooth(fine_iter + freedom * prolong(mid_iter, fine_mid, moves), rhs_fine, apply_fine, inverse_fine, SWEEPS)
    return fine_iter, rhs_fine - apply_fine(fine_iter)


def loop_shift(values, upward):
    axis = values.ndim - 3
    zeros = jnp.zeros_like(lax.slice_in_dim(values, 0, 1, axis=axis))
    if upward:
        return jnp.concatenate([lax.slice_in_dim(values, 1, N_GROUP, axis=axis), zeros], axis=axis)
    return jnp.concatenate([zeros, lax.slice_in_dim(values, 0, N_GROUP - 1, axis=axis)], axis=axis)


def reference(load, stiffness_dir, bulk_ratio, thermal_shift, contact, loop_tie):
    layout = (N_GROUP, N_MEMBER, E_DEV)

    def cells(values):
        return values.reshape(values.shape[:-1] + layout)

    def along_next(values):
        return jnp.roll(values, -1, axis=-2)

    def along_prev(values):
        return jnp.roll(values, 1, axis=-2)

    def across_next(values):
        return jnp.roll(values, -1, axis=-1)

    def across_prev(values):
        return jnp.roll(values, 1, axis=-1)

    moves = (along_next, across_next, along_prev, across_prev)
    coefficients = (cells(stiffness_dir), cells(bulk_ratio), cells(thermal_shift))
    freedom = free_mask(cells(contact).astype(jnp.float32), NODES)
    loop_index = lax.broadcasted_iota(jnp.int32, layout, 0)
    tie_live = jnp.where(loop_index < N_GROUP - 1, cells(loop_tie), jnp.float32(0.0))
    tie_under = loop_shift(tie_live, False)

    def apply_coarse(values):
        return level_apply(values, coefficients, COARSE_NODES, moves) + tie_live * (values - loop_shift(values, True)) + tie_under * (values - loop_shift(values, False))

    inverse_coarse = 1.0 / (level_diagonal(coefficients, COARSE_NODES, moves) + tie_live + tie_under)

    def coarse_solve(rhs):
        return chebyshev(rhs, apply_coarse, inverse_coarse)

    solution, residual = vcycle(cells(load), coefficients, freedom, moves, coarse_solve)
    return solution.reshape(load.shape), residual.reshape(load.shape)
```

```python
import functools

import jax
import jax.numpy as jnp
import numpy as np
from jax import lax
from jax.experimental import pallas as pl
from jax.experimental.pallas import tpu as pltpu
from jax.sharding import PartitionSpec as P

NODES = 8
MID_NODES = 4
COARSE_NODES = 2
SWEEPS = 2
CHEB = 6
OMEGA = 0.3
LOWER_BOUND = 0.3
UPPER_BOUND = 3.0
LANES = 128
SUB = 8
VMEM_LIMIT = 6 * 1024 * 1024


def tables(resolution):
    indices = np.arange(resolution)
    points = -np.cos(np.pi * indices / (resolution - 1))
    padded = np.concatenate([points[:1], points, points[-1:]])
    weights = (padded[2:] - padded[:-2]) / 2.0
    factor = np.where((indices == 0) | (indices == resolution - 1), 2.0, 1.0)
    spacing = points[:, None] - points[None, :] + np.eye(resolution)
    parity = np.where((indices[:, None] + indices[None, :]) % 2 == 0, 1.0, -1.0)
    offdiag = (1.0 - np.eye(resolution)) * factor[:, None] / factor[None, :] * parity / spacing
    derivative = offdiag - np.eye(resolution) * offdiag.sum(axis=1)[:, None]
    diagonal = (weights[:, None] * derivative * derivative).sum(axis=0)
    stiffness = derivative.T @ (weights[:, None] * derivative)
    return points, weights, stiffness, diagonal


def interpolation(fine_count, coarse_count):
    fine_points = tables(fine_count)[0]
    coarse_points = tables(coarse_count)[0]
    columns = []
    for column in range(coarse_count):
        values = np.ones(fine_count)
        for partner in range(coarse_count):
            if partner != column:
                values = (
                    values
                    * (fine_points - coarse_points[partner])
                    / (coarse_points[column] - coarse_points[partner])
                )
        columns.append(values)
    return np.stack(columns, axis=1)


_, W8, S8, G8 = tables(NODES)
_, W4, S4, G4 = tables(MID_NODES)
_, W2, S2, G2 = tables(COARSE_NODES)
J84 = interpolation(NODES, MID_NODES)
J42 = interpolation(MID_NODES, COARSE_NODES)


def rolled(matrix):
    row = np.arange(SUB)
    return [matrix[row, (row - j) % SUB] for j in range(SUB)]


def embed(matrix):
    out = np.zeros((SUB, SUB))
    out[: matrix.shape[0], : matrix.shape[1]] = matrix
    return out


def column(values):
    out = np.zeros(SUB)
    out[: len(values)] = values
    return out


TABLE_ROWS = {}
_rows = []


def _add(name, rows):
    TABLE_ROWS[name] = (len(_rows), len(rows))
    _rows.extend(rows)


_add("k8", rolled(S8))
_add("k4", rolled(embed(S4)))
_add("r84", rolled(embed(J84.T)))
_add("p84", rolled(embed(J84)))
_add("w8", [column(W8)])
_add("g8", [column(G8)])
_add("w4", [column(W4)])
_add("g4", [column(G4)])
_add("pad4", [1.0 - column(np.ones(MID_NODES))])
_add("j42", [column(J42[:, 0]), column(J42[:, 1])])
TABLE = np.broadcast_to(
    np.stack(_rows)[:, :, None], (len(_rows), SUB, LANES)
).astype(np.float32)


def table(ref, name):
    start, count = TABLE_ROWS[name]
    rows = [ref[start + i] for i in range(count)]
    return rows if count > 1 else rows[0]


def scalar(value):
    return np.float32(value)


def lane_next(value):
    return pltpu.roll(value, LANES - 1, 1)


def lane_prev(value):
    return pltpu.roll(value, 1, 1)


def combine(factors, values):
    total = None
    for factor, value in zip(factors, values):
        if float(factor) == 0.0:
            continue
        term = value if float(factor) == 1.0 else scalar(factor) * value
        total = term if total is None else total + term
    return total


def even_odd(matrix, values):
    count = len(values)
    half = count // 2
    even = [values[i] + values[count - 1 - i] for i in range(half)]
    odd = [values[i] - values[count - 1 - i] for i in range(half)]
    front, back = [], []
    for i in range(half):
        sym = [(matrix[i, j] + matrix[i, count - 1 - j]) / 2.0 for j in range(half)]
        anti = [(matrix[i, j] - matrix[i, count - 1 - j]) / 2.0 for j in range(half)]
        e = combine(sym, even)
        o = combine(anti, odd)
        front.append(e + o)
        back.append(e - o)
    return front + back[::-1]


def along_sublanes(factors, value, offsets=range(SUB)):
    total = None
    for j in offsets:
        moved = value if j == 0 else pltpu.roll(value, j, 0)
        term = factors[j] * moved
        total = term if total is None else total + term
    return total


MID_OFFSETS = (0, 1, 2, 3, 5, 6, 7)


class Coefs:
    def __init__(self, rows):
        self.s = [rows[i : i + 1] for i in range(3)]
        self.bulk = rows[3:4]
        self.shift = rows[4:5]

    def alphas(self):
        extra = 1.0 + self.bulk / 3.0
        return [extra * self.s[0], extra * self.s[1], extra * self.s[2], self.shift]


def inverse_diagonal(own, prev, nxt, weight, slope, w_k, g_k, pad):
    count = len(weight)

    def block(alphas, a, b):
        al1, al2, al3, sh = alphas
        return scalar(weight[b]) * (scalar(slope[a]) * al1 * w_k) + scalar(weight[a]) * (
            scalar(slope[b]) * al2 * w_k + scalar(weight[b]) * (al3 * g_k + sh * w_k)
        )

    sets = {0: [p + q for p, q in zip(own, prev)], count - 1: [p + q for p, q in zip(own, nxt)]}
    result = []
    for a in range(count):
        alphas = sets.get(a, own)
        folded = [p + lane_prev(jnp.broadcast_to(p, (SUB, LANES)))[0:1] for p in alphas]
        line = []
        for b in range(count - 1):
            value = block(folded if b == 0 else alphas, a, b)
            if pad is not None:
                value = value + pad
            line.append(scalar(OMEGA) / value)
        result.append(line)
    return result


def fine_mix(own, d_ref, v_ref, a, values):
    third = own.bulk * scalar(1.0 / 3.0)
    for b in range(NODES - 1):
        trio = [values[c][b] for c in range(3)]
        mean = third * (trio[0] + trio[1] + trio[2])
        for c in range(3):
            d_ref[c, a, b] = trio[c]
            v_ref[c, a, b] = trio[c] + mean
        if b == 0:
            trio = [lane_next(v) for v in trio]
            mean = third * (trio[0] + trio[1] + trio[2])
            for c in range(3):
                d_ref[c, a, NODES - 1] = trio[c]
                v_ref[c, a, NODES - 1] = trio[c] + mean


def fine_apply(tbl, own, d_ref, v_ref, acc_ref, c, emit):
    w_k = table(tbl, "w8")
    k8 = table(tbl, "k8")
    t1 = own.s[0] * w_k
    t2 = own.s[1] * w_k
    t3 = jnp.broadcast_to(own.s[2], (SUB, LANES))
    tq = own.shift * w_k
    scaled = S8 / W8[:, None]
    for b in range(NODES):
        outs = even_odd(scaled, [v_ref[c, a, b] for a in range(NODES)])
        for a in range(NODES):
            acc_ref[a, b] = t1 * outs[a]
    for a in range(NODES):
        line = [v_ref[c, a, b] for b in range(NODES)]
        outs = even_odd(scaled, line)
        ys = []
        for b in range(NODES):
            kd = along_sublanes(k8, line[b])
            value = acc_ref[a, b] + t2 * outs[b] + t3 * kd + tq * d_ref[c, a, b]
            ys.append(scalar(W8[a] * W8[b]) * value)
        ys[0] = ys[0] + lane_prev(ys[NODES - 1])
        for b in range(NODES - 1):
            emit(a, b, ys[b])


def fine_inverse(tbl, own, prev, nxt, contact_ref, face_contact, inv_ref):
    w_k, g_k = table(tbl, "w8"), table(tbl, "g8")
    inverse = inverse_diagonal(
        own.alphas(), prev.alphas(), nxt.alphas(), W8, G8, w_k, g_k, None
    )
    level = lax.broadcasted_iota(jnp.int32, (SUB, LANES), 0)
    for a in range(NODES):
        for b in range(NODES - 1):
            if a < NODES - 1:
                low = 1.0 - contact_ref[0, a, b : b + 1].astype(jnp.float32)
                high = 1.0 - contact_ref[1, a, b : b + 1].astype(jnp.float32)
            else:
                low = 1.0 - face_contact[0][b : b + 1]
                high = 1.0 - face_contact[1][b : b + 1]
            free = jnp.where(level == 0, low, jnp.where(level == NODES - 1, high, scalar(1.0)))
            inv_ref[a, b] = free * inverse[a][b]


def first_fine_kernel(
    tbl, load, contact, coefs, from_next, from_prev, inv, x, r, lo, hi, d_ref, v_ref, acc_ref
):
    own = Coefs(coefs[...])
    nxt = Coefs(from_next[23])
    prev = Coefs(from_prev[0])
    fine_inverse(tbl, own, prev, nxt, contact, (from_next[21], from_next[22]), inv)
    for c in range(3):
        for a in range(NODES - 1):
            for b in range(NODES - 1):
                r[c, a, b] = load[c, a, b]
        for b in range(NODES - 1):
            r[c, NODES - 1, b] = from_next[c * (NODES - 1) + b]

    def mix(a, carry):
        values = [[inv[a, b] * r[c, a, b] for b in range(NODES - 1)] for c in range(3)]
        fine_mix(own, d_ref, v_ref, a, values)
        return carry

    lax.fori_loop(0, NODES, mix, 0)

    def apply(c, carry):
        def emit(a, b, y):
            r[c, a, b] = r[c, a, b] - y
            if a == 0:
                lo[c, b] = y
            if a == NODES - 1:
                hi[c, b] = y
            else:
                x[c, a, b] = d_ref[c, a, b]

        fine_apply(tbl, own, d_ref, v_ref, acc_ref, c, emit)
        return carry

    lax.fori_loop(0, 3, apply, 0)


def fine_correct(own, r_in, inv, x_in, x, r, from_prev, from_next, d_ref, v_ref):
    def copy(c, carry):
        for b in range(NODES - 1):
            r[c, 0, b] = r_in[c, 0, b] - from_prev[c, b]
            r[c, NODES - 1, b] = r_in[c, NODES - 1, b] - from_next[c, b]
        return carry

    lax.fori_loop(0, 3, copy, 0)

    def layer(a, source):
        values = [[inv[a, b] * source[c, a, b] for b in range(NODES - 1)] for c in range(3)]
        fine_mix(own, d_ref, v_ref, a, values)
        return values

    def add(a, values):
        for c in range(3):
            for b in range(NODES - 1):
                x[c, a, b] = x_in[c, a, b] + values[c][b]

    add(0, layer(0, r))
    layer(NODES - 1, r)

    def inner(a, carry):
        add(a, layer(a, r_in))
        return carry

    lax.fori_loop(1, NODES - 1, inner, 0)


def fine_subtract(r_in, r, c, a, b, y):
    source = r if a in (0, NODES - 1) else r_in
    r[c, a, b] = source[c, a, b] - y


def second_fine_kernel(
    tbl, coefs, inv, x_in, r_in, from_prev, from_next, x, r, lo, hi, low, d_ref, v_ref, acc_ref
):
    own = Coefs(coefs[...])
    fine_correct(own, r_in, inv, x_in, x, r, from_prev, from_next, d_ref, v_ref)

    def apply(c, carry):
        def emit(a, b, y):
            fine_subtract(r_in, r, c, a, b, y)
            if a == 0:
                lo[c, b] = y
            if a == NODES - 1:
                hi[c, b] = y

        fine_apply(tbl, own, d_ref, v_ref, acc_ref, c, emit)

        lines = [[None] * (NODES - 1) for _ in range(MID_NODES)]
        for b in range(NODES - 1):
            parts = []
            for a in range(NODES):
                part = r[c, a, b] if a < NODES - 1 else -hi[c, b]
                parts.append(jnp.where(inv[a, b] > 0.0, part, scalar(0.0)))
            for i in range(MID_NODES):
                lines[i][b] = combine(J84[:, i], parts)
        r84 = table(tbl, "r84")
        for i in range(MID_NODES):
            outs = []
            for j in range(MID_NODES):
                outs.append(along_sublanes(r84, combine(J84[: NODES - 1, j], lines[i])))
            outs[0] = outs[0] + lane_prev(outs[MID_NODES - 1])
            for j in range(MID_NODES - 1):
                low[c, i, j] = outs[j]
        return carry

    lax.fori_loop(0, 3, apply, 0)


def sweep_fine_kernel(
    tbl, coefs, inv, x_in, r_in, from_prev, from_next, x, r, lo, hi, d_ref, v_ref, acc_ref
):
    own = Coefs(coefs[...])
    fine_correct(own, r_in, inv, x_in, x, r, from_prev, from_next, d_ref, v_ref)

    def apply(c, carry):
        def emit(a, b, y):
            fine_subtract(r_in, r, c, a, b, y)
            if a == 0 and lo is not None:
                lo[c, b] = y
            if a == NODES - 1:
                hi[c, b] = y

        fine_apply(tbl, own, d_ref, v_ref, acc_ref, c, emit)
        return carry

    lax.fori_loop(0, 3, apply, 0)


def last_sweep_kernel(
    tbl, coefs, inv, x_in, r_in, from_prev, from_next, x, r, hi, d_ref, v_ref, acc_ref
):
    sweep_fine_kernel(
        tbl, coefs, inv, x_in, r_in, from_prev, from_next, x, r, None, hi, d_ref, v_ref, acc_ref
    )


def final_kernel(inv, r_in, from_prev, out):
    def body(c, carry):
        for a in range(NODES - 1):
            for b in range(NODES - 1):
                value = r_in[c, a, b]
                if a == 0:
                    value = value - from_prev[c, b]
                out[c, a, b] = jnp.where(inv[a, b] > 0.0, value, scalar(0.0))
        return carry

    lax.fori_loop(0, 3, body, 0)


def mid_apply(tbl, own, d):
    n = MID_NODES
    w_k, k4 = table(tbl, "w4"), table(tbl, "k4")
    t1 = own.s[0] * w_k
    t2 = own.s[1] * w_k
    t3 = jnp.broadcast_to(own.s[2], (SUB, LANES))
    tq = own.shift * w_k
    third = own.bulk * scalar(1.0 / 3.0)
    scaled = S4 / W4[:, None]
    full = [[d[c][a] + [lane_next(d[c][a][0])] for a in range(n)] for c in range(3)]
    mix = [[[None] * n for _ in range(n)] for _ in range(3)]
    for a in range(n):
        for b in range(n):
            mean = third * (full[0][a][b] + full[1][a][b] + full[2][a][b])
            for c in range(3):
                mix[c][a][b] = full[c][a][b] + mean
    result = []
    for c in range(3):
        first = [even_odd(scaled, [mix[c][a][b] for a in range(n)]) for b in range(n)]
        layers = []
        for a in range(n):
            second = even_odd(scaled, mix[c][a])
            ys = []
            for b in range(n):
                kd = along_sublanes(k4, mix[c][a][b], MID_OFFSETS)
                value = t1 * first[b][a] + t2 * second[b] + t3 * kd + tq * full[c][a][b]
                ys.append(scalar(W4[a] * W4[b]) * value)
            ys[0] = ys[0] + lane_prev(ys[n - 1])
            layers.append(ys[: n - 1])
        result.append(layers)
    return result


def mid_read(ref):
    return [
        [[ref[c, a, b] for b in range(MID_NODES - 1)] for a in range(MID_NODES)] for c in range(3)
    ]


def mid_write(ref, values):
    for c in range(3):
        for a in range(MID_NODES):
            for b in range(MID_NODES - 1):
                ref[c, a, b] = values[c][a][b]


def mid_map(function, *values):
    return [
        [
            [function(*(v[c][a][b] for v in values)) for b in range(MID_NODES - 1)]
            for a in range(MID_NODES)
        ]
        for c in range(3)
    ]


def mid_faces(values, from_prev, from_next, sign):
    for c in range(3):
        for b in range(MID_NODES - 1):
            values[c][0][b] = values[c][0][b] + sign * from_prev[c, b]
            values[c][MID_NODES - 1][b] = values[c][MID_NODES - 1][b] + sign * from_next[c, b]
    return values


def mid_scale(inv, values):
    return [
        [[inv[a, b] * values[c][a][b] for b in range(MID_NODES - 1)] for a in range(MID_NODES)]
        for c in range(3)
    ]


def write_faces(values, lo, hi, add=None):
    for c in range(3):
        for b in range(MID_NODES - 1):
            low, high = values[c][0][b], values[c][MID_NODES - 1][b]
            if add is not None:
                low, high = low + add[0][c, b], high + add[1][c, b]
            lo[c, b] = low
            hi[c, b] = high


def minus(p, q):
    return p - q


def plus(p, q):
    return p + q


def first_mid_kernel(
    tbl, coefs, coefs_next, coefs_prev, b_in, from_prev, from_next, inv, x, r, lo, hi
):
    own = Coefs(coefs[...])
    nxt = Coefs(coefs_next[23])
    prev = Coefs(coefs_prev[0])
    inverse = inverse_diagonal(
        own.alphas(),
        prev.alphas(),
        nxt.alphas(),
        W4,
        G4,
        table(tbl, "w4"),
        table(tbl, "g4"),
        table(tbl, "pad4"),
    )
    for a in range(MID_NODES):
        for b in range(MID_NODES - 1):
            inv[a, b] = inverse[a][b]
    rhs = mid_faces(mid_read(b_in), from_prev, from_next, 1.0)
    step = mid_scale(inv, rhs)
    mid_write(x, step)
    y = mid_apply(tbl, own, step)
    mid_write(r, mid_map(minus, rhs, y))
    write_faces(y, lo, hi)


def second_mid_kernel(
    tbl, coefs, inv, x_in, r_in, from_prev, from_next, x, r, lo, hi, send, rows_ref
):
    own = Coefs(coefs[...])
    n = MID_NODES
    remain = mid_faces(mid_read(r_in), from_prev, from_next, -1.0)
    step = mid_scale(inv, remain)
    mid_write(x, mid_map(plus, mid_read(x_in), step))
    y = mid_apply(tbl, own, step)
    rest = mid_map(minus, remain, y)
    mid_write(r, rest)
    write_faces(y, lo, hi)
    j42 = table(tbl, "j42")
    for c in range(3):
        layers = [rest[c][a] for a in range(n - 1)] + [[-v for v in y[c][n - 1]]]
        for i in range(COARSE_NODES):
            line = [
                combine(J42[:, i], [layers[a][b] for a in range(n)]) for b in range(n - 1)
            ]
            ends = [combine(J42[: n - 1, j], line) for j in range(COARSE_NODES)]
            total = ends[0] + lane_prev(ends[1])
            for k in range(COARSE_NODES):
                row = (i * 3 + c) * COARSE_NODES + k
                rows_ref[row : row + 1] = jnp.sum(j42[k] * total, axis=0, keepdims=True)
    rows_ref[12:18] = coefs[...]
    block = rows_ref[...]

    def spread(i, carry):
        send[i] = block
        return carry

    lax.fori_loop(0, send.shape[0], spread, 0)


def third_mid_kernel(
    tbl, coefs, r_in, lo_in, hi_in, coarse, e, r, lo, hi
):
    own = Coefs(coefs[...])
    n = MID_NODES
    j42 = table(tbl, "j42")
    step = []
    for c in range(3):
        ends = []
        for i in range(COARSE_NODES):
            total = None
            for k in range(COARSE_NODES):
                row = (i * 3 + c) * COARSE_NODES + k
                term = j42[k] * coarse[row : row + 1]
                total = term if total is None else total + term
            ends.append(total)
        layers = []
        for a in range(n):
            near = combine(J42[a], ends)
            far = lane_next(near)
            layers.append([combine(J42[b], [near, far]) for b in range(n - 1)])
        step.append(layers)
    mid_write(e, step)
    y = mid_apply(tbl, own, step)
    mid_write(r, mid_map(minus, mid_read(r_in), y))
    write_faces(y, lo, hi, (lo_in, hi_in))


def sweep_mid_kernel(tbl, coefs, inv, x_in, e_in, r_in, from_prev, from_next, x, r, lo, hi):
    own = Coefs(coefs[...])
    remain = mid_faces(mid_read(r_in), from_prev, from_next, -1.0)
    step = mid_scale(inv, remain)
    total = mid_map(plus, mid_map(plus, mid_read(x_in), mid_read(e_in)), step)
    mid_write(x, total)
    y = mid_apply(tbl, own, step)
    mid_write(r, mid_map(minus, remain, y))
    write_faces(y, lo, hi)


def up_kernel(
    tbl, coefs, inv_mid, x_mid, r_mid, mid_prev, mid_next,
    inv, x_in, r_in, lo_in, hi_in, x, r, lo, hi, d_ref, v_ref, acc_ref, up_ref,
):
    own = Coefs(coefs[...])
    remain = mid_faces(mid_read(r_mid), mid_prev, mid_next, -1.0)
    total = mid_map(plus, mid_read(x_mid), mid_scale(inv_mid, remain))
    p84 = table(tbl, "p84")
    for c in range(3):
        for i in range(MID_NODES):
            for j in range(MID_NODES - 1):
                value = along_sublanes(p84, total[c][i][j])
                up_ref[c, i, j] = value
                if j == 0:
                    up_ref[c, i, MID_NODES - 1] = lane_next(value)

    def rise(c, carry):
        for j in range(MID_NODES):
            line = [up_ref[c, i, j] for i in range(MID_NODES)]
            for a in range(NODES):
                acc_ref[a, j] = combine(J84[a], line)
        for a in range(NODES):
            line = [acc_ref[a, j] for j in range(MID_NODES)]
            for b in range(NODES - 1):
                value = jnp.where(inv[a, b] > 0.0, combine(J84[b], line), scalar(0.0))
                d_ref[c, a, b] = value
                if a < NODES - 1:
                    x[c, a, b] = x_in[c, a, b] + value
        return carry

    lax.fori_loop(0, 3, rise, 0)

    def mix(a, carry):
        values = [[d_ref[c, a, b] for b in range(NODES - 1)] for c in range(3)]
        fine_mix(own, d_ref, v_ref, a, values)
        return carry

    lax.fori_loop(0, NODES, mix, 0)

    def apply(c, carry):
        def emit(a, b, y):
            r[c, a, b] = r_in[c, a, b] - y
            if a == 0:
                lo[c, b] = y + lo_in[c, b]
            if a == NODES - 1:
                hi[c, b] = y + hi_in[c, b]

        fine_apply(tbl, own, d_ref, v_ref, acc_ref, c, emit)
        return carry

    lax.fori_loop(0, 3, apply, 0)


def coarse_kernel(loops, place, gathered, out, coef_ref, keep_ref):
    members = gathered.shape[0] // loops

    def pick(g, row):
        return gathered[g * members : (g + 1) * members, row, :]

    def up_member(v):
        return pltpu.roll(v, members - 1, 0)

    def down_member(v):
        return pltpu.roll(v, 1, 0)

    def fold(parts):
        near = [parts[i][0] + lane_prev(parts[i][1]) for i in range(2)]
        return near[0] + down_member(near[1])

    half = scalar(0.5)
    ties, inverse, rhs = [], [], []
    for g in range(loops):
        ties.append(pick(g, 17) if g + 1 < loops else None)
    for g in range(loops):
        rows = [pick(g, 12 + i) for i in range(5)]
        third = rows[3] / 3.0
        extra = 1.0 + third
        diag = extra * (half * (rows[0] + rows[1] + rows[2])) + rows[4]
        total = fold([[diag, diag], [diag, diag]])
        if ties[g] is not None:
            total = total + ties[g]
        if g > 0:
            total = total + ties[g - 1]
        inverse.append(1.0 / total)
        for i in range(3):
            coef_ref[g, i] = half * rows[i]
        coef_ref[g, 3] = third
        coef_ref[g, 4] = rows[4]
        line = []
        for c in range(3):
            for k in range(2):
                low = pick(g, c * 2 + k)
                high = pick(g, 6 + c * 2 + k)
                line.append(low + down_member(high))
        rhs.append(line)

    def operator(u):
        result = []
        for g in range(loops):
            s1, s2, s3, third, shift = [coef_ref[g, i] for i in range(5)]
            full = [[None, None], [None, None]]
            for i in range(2):
                base = u[g] if i == 0 else [up_member(v) for v in u[g]]
                full[i][0] = base
                full[i][1] = [lane_next(v) for v in base]
            mix = [[None, None], [None, None]]
            for i in range(2):
                for j in range(2):
                    f = full[i][j]
                    means = [third * (f[k] + f[2 + k] + f[4 + k]) for k in range(2)]
                    mix[i][j] = [f[c * 2 + k] + means[k] for c in range(3) for k in range(2)]
            line = []
            for c in range(3):
                slope = {}
                for j in range(2):
                    for k in range(2):
                        slope[0, j, k] = s1 * (mix[0][j][c * 2 + k] - mix[1][j][c * 2 + k])
                for i in range(2):
                    for k in range(2):
                        slope[1, i, k] = s2 * (mix[i][0][c * 2 + k] - mix[i][1][c * 2 + k])
                for i in range(2):
                    for j in range(2):
                        slope[2, i, j] = s3 * (mix[i][j][c * 2] - mix[i][j][c * 2 + 1])
                for k in range(2):
                    parts = [[None, None], [None, None]]
                    for i in range(2):
                        for j in range(2):
                            value = shift * full[i][j][c * 2 + k]
                            p, q, t = slope[0, j, k], slope[1, i, k], slope[2, i, j]
                            value = value + p if i == 0 else value - p
                            value = value + q if j == 0 else value - q
                            value = value + t if k == 0 else value - t
                            parts[i][j] = value
                    total = fold(parts)
                    own = u[g][c * 2 + k]
                    if ties[g] is not None:
                        total = total + ties[g] * (own - u[g + 1][c * 2 + k])
                    if g > 0:
                        total = total + ties[g - 1] * (own - u[g - 1][c * 2 + k])
                    line.append(total)
            result.append(line)
        return result

    center = 0.5 * (UPPER_BOUND + LOWER_BOUND)
    radius = 0.5 * (UPPER_BOUND - LOWER_BOUND)
    ratio = center / radius
    damping_now = 1.0 / ratio
    each = [(g, i) for g in range(loops) for i in range(6)]
    remain = rhs
    update = [[inverse[g] * remain[g][i] / scalar(center) for i in range(6)] for g in range(loops)]
    for g, i in each:
        keep_ref[g, i] = update[g][i]
    for iteration in range(CHEB - 1):
        product = operator(update)
        remain = [[remain[g][i] - product[g][i] for i in range(6)] for g in range(loops)]
        damping_next = 1.0 / (2.0 * ratio - damping_now)
        lead = scalar(damping_next * damping_now)
        gain = scalar(2.0 * damping_next / radius)
        update = [
            [lead * update[g][i] + (gain * inverse[g]) * remain[g][i] for i in range(6)]
            for g in range(loops)
        ]
        for g, i in each:
            keep_ref[g, i] = keep_ref[g, i] + update[g][i]
        damping_now = damping_next
    group = place[0]
    here = place[1]
    above = place[2]
    for i in range(6):
        out[i : i + 1] = keep_ref[group, i, pl.ds(here, 1), :]
        out[6 + i : 7 + i] = keep_ref[group, i, pl.ds(above, 1), :]


VMEM = pl.BlockSpec(memory_space=pltpu.VMEM)
SMEM = pl.BlockSpec(memory_space=pltpu.SMEM)


def shape(*dims):
    return jax.ShapeDtypeStruct(dims, jnp.float32)


FINE = (3, NODES, NODES - 1, SUB, LANES)
OWNED = (3, NODES - 1, NODES - 1, SUB, LANES)
FINE_FACE = (3, NODES - 1, SUB, LANES)
MID = (3, MID_NODES, MID_NODES - 1, SUB, LANES)
MID_FACE = (3, MID_NODES - 1, SUB, LANES)
FINE_SCRATCH = (
    pltpu.VMEM((3, NODES, NODES, SUB, LANES), jnp.float32),
    pltpu.VMEM((3, NODES, NODES, SUB, LANES), jnp.float32),
    pltpu.VMEM((NODES, NODES, SUB, LANES), jnp.float32),
)


def call(kernel, outs, scratch, *args, specs=None, limit=VMEM_LIMIT):
    return pl.pallas_call(
        kernel,
        out_shape=tuple(shape(*o) for o in outs),
        in_specs=specs or [VMEM] * len(args),
        out_specs=tuple([VMEM] * len(outs)),
        scratch_shapes=list(scratch),
        compiler_params=pltpu.CompilerParams(vmem_limit_bytes=limit),
    )(*args)


def ring(values, by):
    size = lax.axis_size("member")
    return lax.ppermute(values, "member", [(i, (i + by) % size) for i in range(size)])


def exchange(lo, hi):
    from_next = ring(lo, -1)
    from_prev = ring(hi, 1)
    return from_prev, from_next


def body(load, stiffness_dir, bulk_ratio, thermal_shift, contact, loop_tie):
    loops = lax.axis_size("group")
    members = lax.axis_size("member")
    devices = loops * members
    tbl = jnp.asarray(TABLE)
    coefs = jnp.concatenate(
        [stiffness_dir, bulk_ratio[None], thermal_shift[None], loop_tie[None]], axis=0
    )
    padded = jnp.pad(coefs, ((0, SUB - 6), (0, 0)))[None]
    faces = jnp.pad(contact[:, 0].astype(jnp.float32), ((0, 0), (0, 1), (0, 0)))
    down = jnp.concatenate(
        [load[:, 0].reshape(3 * (NODES - 1), SUB, LANES), faces, padded], axis=0
    )
    first_next = ring(down, -1)
    first_prev = ring(padded, 1)

    inv, x, r, lo, hi = call(
        first_fine_kernel,
        (FINE[1:], OWNED, FINE, FINE_FACE, FINE_FACE),
        FINE_SCRATCH,
        tbl, load, contact, coefs, first_next, first_prev,
    )
    from_prev, from_next = exchange(lo, hi)
    x, r, lo, hi, low = call(
        second_fine_kernel,
        (OWNED, FINE, FINE_FACE, FINE_FACE, MID),
        FINE_SCRATCH,
        tbl, coefs, inv, x, r, from_prev, from_next,
    )
    from_prev, from_next = exchange(low[:, 0], low[:, MID_NODES - 1])
    inv_mid, x_mid, r_mid, mid_lo, mid_hi = call(
        first_mid_kernel,
        (MID[1:], MID, MID, MID_FACE, MID_FACE),
        (),
        tbl, coefs, first_next, first_prev, low, from_prev, from_next,
    )
    from_prev, from_next = exchange(mid_lo, mid_hi)
    x_mid, r_mid, mid_lo, mid_hi, send = call(
        second_mid_kernel,
        (MID, MID, MID_FACE, MID_FACE, (devices, 18, LANES)),
        (pltpu.VMEM((18, LANES), jnp.float32),),
        tbl, coefs, inv_mid, x_mid, r_mid, from_prev, from_next,
    )
    gathered = lax.all_to_all(send, ("group", "member"), 0, 0)
    me = lax.axis_index("member")
    place = jnp.stack(
        [lax.axis_index("group"), me, jnp.where(me + 1 == members, 0, me + 1)]
    ).astype(jnp.int32)
    (coarse,) = call(
        functools.partial(coarse_kernel, loops),
        ((12, LANES),),
        (
            pltpu.VMEM((loops, 5, members, LANES), jnp.float32),
            pltpu.VMEM((loops, 6, members, LANES), jnp.float32),
        ),
        place, gathered,
        specs=[SMEM, VMEM],
        limit=max(VMEM_LIMIT, devices * 64 * 1024),
    )
    e_mid, r_mid, mid_lo, mid_hi = call(
        third_mid_kernel,
        (MID, MID, MID_FACE, MID_FACE),
        (),
        tbl, coefs, r_mid, mid_lo, mid_hi, coarse,
    )
    from_prev, from_next = exchange(mid_lo, mid_hi)
    x_mid, r_mid, mid_lo, mid_hi = call(
        sweep_mid_kernel,
        (MID, MID, MID_FACE, MID_FACE),
        (),
        tbl, coefs, inv_mid, x_mid, e_mid, r_mid, from_prev, from_next,
    )
    from_prev, from_next = exchange(mid_lo, mid_hi)
    x, r, lo, hi = call(
        up_kernel,
        (OWNED, FINE, FINE_FACE, FINE_FACE),
        FINE_SCRATCH + (pltpu.VMEM((3, MID_NODES, MID_NODES, SUB, LANES), jnp.float32),),
        tbl, coefs, inv_mid, x_mid, r_mid, from_prev, from_next, inv, x, r, lo, hi,
    )
    from_prev, from_next = exchange(lo, hi)
    x, r, lo, hi = call(
        sweep_fine_kernel,
        (OWNED, FINE, FINE_FACE, FINE_FACE),
        FINE_SCRATCH,
        tbl, coefs, inv, x, r, from_prev, from_next,
    )
    from_prev, from_next = exchange(lo, hi)
    x, r, hi = call(
        last_sweep_kernel,
        (OWNED, FINE, FINE_FACE),
        FINE_SCRATCH,
        tbl, coefs, inv, x, r, from_prev, from_next,
    )
    (residual,) = call(final_kernel, (OWNED,), (), inv, r, ring(hi, 1))
    return x, residual


def solution(mesh):
    in_specs = (
        P(None, None, None, None, ("group", "member")),
        P(None, ("group", "member")),
        P(("group", "member")),
        P(("group", "member")),
        P(None, None, None, ("group", "member")),
        P(("group", "member")),
    )
    out_specs = (
        P(None, None, None, None, ("group", "member")),
        P(None, None, None, None, ("group", "member")),
    )
    return jax.shard_map(body, mesh=mesh, in_specs=in_specs, out_specs=out_specs, check_vma=False)
```
